32 devices in a mesh: row: 2 (over y), col: 16 (over z, x, core).
Axes of the slice: x: 2, y: 2, z: 4, core: 2. Of those that a mesh axis runs over, the one named last changes fastest.
Arguments:
- start_block: float32 [32, 8192], P(None, 'col'), may hold values from -6 to 6
- energies: float32 [8192], P('col'), may hold values from 1 to 10
- hamiltonian: float32 [16, 16, 512, 512], P('row', 'col'), may hold values from -0.125 to 0.125
Outputs:
- recurrence: float32 [2, 2, 32, 32], replicated
- next_block: float32 [32, 8192], P(None, 'col')
The draws below stay inside these ranges and needn't reach their ends.
All inputs are finite; a program needn't handle non-finite values.
Results may differ from the reference program's by a relative error of at most 0.0003.
Values sent between devices are 32-bit elements; how exact they have to be, the bound alone decides.
A program may use at most 64 MiB of HBM per device.

```python
import math
import jax
import jax.numpy as jnp
from jax import lax

VECS = 32
BLK = 512
ITERS = 2
NBLK = 16
N = 8192
N_ROW = 2


def block_scale(own_key, dims, split, smallest, top_value):
    gain, own = 1.0, jax.random.fold_in(own_key, 6)
    for position, parts in split:
        heights = jnp.exp(jax.random.uniform(jax.random.fold_in(own, position), (parts,), jnp.float32, smallest / len(split), top_value / len(split)))
        gain = gain * jnp.repeat(heights, dims[position] // parts).reshape([-1 if axis == position else 1 for axis in range(len(dims))])
    return gain


def bell_draw(own_key, shape, deviation, reach, split=(), held_as=jnp.bfloat16):
    factor_of = block_scale(own_key, shape, split, -0.22, 0.18) if split else 1.0
    entries = jax.random.normal(own_key, shape, jnp.float32) * deviation * factor_of
    return jnp.minimum(jnp.maximum(entries, -reach), reach).astype(held_as)


def setup_inputs(seed: int = 0) -> dict:
    arg_keys = jax.random.split(jax.random.key(seed), 4)
    start_block = bell_draw(arg_keys[0], (VECS, N), 1.0, 6.0, ((1, 16),), jnp.float32)
    energies = jnp.clip(jnp.exp(math.log(10.0) - 2.3025851 * jax.random.uniform(arg_keys[1], (N,), jnp.float32) ** block_scale(arg_keys[1], (N,), ((0, 16),), -0.2, 0.2)), 1.0, 10.0)
    hamiltonian = bell_draw(arg_keys[2], (NBLK, NBLK, BLK, BLK), (N // 4) ** -0.5, 0.125, ((0, 2), (1, 16)), jnp.float32)
    return dict(start_block=start_block, energies=energies, hamiltonian=hamiltonian)


FULL_PRECISION = lax.Precision.HIGHEST

def apply_operator(vectors, energies, hamiltonian):
    slot_count = NBLK // N_ROW
    stored = jnp.arange(NBLK, dtype=jnp.int32)
    block_of = (stored % slot_count * N_ROW + stored // slot_count).astype(jnp.int32)
    where_is = (stored % N_ROW * slot_count + stored // N_ROW).astype(jnp.int32)
    by_block = vectors.reshape(VECS, NBLK, BLK).transpose(1, 0, 2)
    in_stored = by_block[block_of]

    def column(running, column_index):
        col_blocks = lax.dynamic_index_in_dim(hamiltonian, column_index, 1, keepdims=False)
        weight = jnp.where(block_of < column_index, jnp.float32(1.0), jnp.where(block_of == column_index, jnp.float32(0.5), jnp.float32(0.0))).astype(jnp.float32)
        downward = jnp.einsum('ipk,ikl->pl', in_stored * weight[:, None, None], col_blocks, precision=FULL_PRECISION)
        own_block = lax.dynamic_index_in_dim(by_block, column_index, 0, keepdims=False)
        across = jnp.einsum('pl,ikl->ipk', own_block, col_blocks, precision=FULL_PRECISION) * weight[:, None, None]
        return (running + across, downward)
    across_total, downs = lax.scan(column, jnp.zeros((NBLK, VECS, BLK), jnp.float32), jnp.arange(NBLK, dtype=jnp.int32))
    summed = downs + across_total[where_is]
    return summed.transpose(1, 0, 2).reshape(VECS, NBLK * BLK) + energies[None, :] * vectors

def mean_inner(left, right):
    return jnp.dot(left, right.T, precision=FULL_PRECISION) / N

def normalize(block):
    factor = jnp.linalg.cholesky(mean_inner(block, block))
    return (lax.linalg.triangular_solve(factor, block, left_side=True, lower=True), factor)

def reference(start_block, energies, hamiltonian):
    current, factor = normalize(start_block)
    previous = jnp.zeros_like(current)
    last_factor = jnp.zeros((VECS, VECS), jnp.float32)
    history = []
    for iteration in range(ITERS):
        residual_block = apply_operator(current, energies, hamiltonian) - jnp.dot(last_factor.T, previous, precision=FULL_PRECISION)
        diagonal_block = mean_inner(residual_block, current)
        residual_block = residual_block - jnp.dot(diagonal_block, current, precision=FULL_PRECISION)
        following, new_factor = normalize(residual_block)
        history.append(jnp.stack([diagonal_block, new_factor]))
        previous, current, last_factor = (current, following, new_factor)
    return (jnp.stack(history), current)
```

```python
import functools

import jax
import jax.numpy as jnp
from jax import lax
from jax.experimental import pallas as pl
from jax.experimental.pallas import tpu as pltpu
from jax.sharding import PartitionSpec as P

ITERS = 2
LANES = 128
MESH = pl.DeviceIdType.MESH
F32 = jnp.float32
BF16 = jnp.bfloat16


def full_dot(left, right, contract):
    return lax.dot_general(
        left, right, (contract, ((), ())), precision=lax.Precision.HIGHEST, preferred_element_type=F32
    )


def split(value):
    high = value.astype(BF16)
    return high, (value - high.astype(F32)).astype(BF16)


def stacked_split(value):
    return jnp.concatenate(split(value), axis=0)


def three_products(stacked, high, low, contract):
    vecs = stacked.shape[0] // 2
    dims = (contract, ((), ()))
    both = lax.dot_general(stacked, high, dims, preferred_element_type=F32)
    extra = lax.dot_general(stacked[:vecs], low, dims, preferred_element_type=F32)
    return both[:vecs] + (both[vecs:] + extra)


def placed_rows(value, slot):
    vecs, width = value.shape
    parts = [jnp.zeros((vecs, width), F32)] * (LANES // vecs)
    parts[slot] = value
    return jnp.concatenate(parts, axis=0)


def factor_and_inverse(gram, row, lane, vecs):
    work = jnp.where(lane < vecs, gram, (lane - vecs == row).astype(F32))
    for step in range(vecs):
        scale = lax.rsqrt(work[step : step + 1, step : step + 1])
        pivot_row = work[step : step + 1, :] * scale
        column = work[:, step : step + 1] * scale
        work = jnp.where(
            row > step, work - column * pivot_row, jnp.where(row == step, pivot_row, work)
        )
    return work


def kernel(
    rows, cols, group,
    x_ref, e_ref, h_ref, rec_ref, next_ref,
    h_buf, h_high, h_low, lhs_buf, w_buf, gathered, across_out, across_in, acc, own, row_parts, gram_one, gram_two,
    h_sem, gather_send, gather_recv, across_send, across_recv, row_send, row_recv, one_send, one_recv, two_send, two_recv,
):
    r, c = lax.axis_index("row"), lax.axis_index("col")
    slots = h_ref.shape[0]
    vecs, width = x_ref.shape
    length = F32(cols * width)
    member, team = c % group, c // group
    teams = cols // group
    is_owner = (c % rows) == r
    row = lax.broadcasted_iota(jnp.int32, (vecs, LANES), 0)
    lane = lax.broadcasted_iota(jnp.int32, (vecs, LANES), 1)

    def remote(src, dst, send, recv, where):
        return pltpu.make_async_remote_copy(
            src_ref=src, dst_ref=dst, send_sem=send, recv_sem=recv, device_id=where, device_id_type=MESH
        )

    def loop(count, start=0):
        def wrap(body):
            lax.fori_loop(start, count, lambda i, _: (body(i), 0)[1], 0)
        return wrap

    def h_copy(i):
        return pltpu.make_async_copy(h_ref.at[i, 0], h_buf.at[i], h_sem.at[i])

    barrier = pltpu.get_barrier_semaphore()

    @loop(cols)
    def _(other):
        @pl.when(other != c)
        def _():
            pl.semaphore_signal(barrier, inc=1, device_id=(r, other), device_id_type=MESH)

    @loop(rows)
    def _(other):
        @pl.when(other != r)
        def _():
            pl.semaphore_signal(barrier, inc=1, device_id=(other, c), device_id_type=MESH)

    @loop(slots)
    def _(i):
        @pl.when(i * rows + r <= c)
        def _():
            h_copy(i).start()

    def one_copy(k, other):
        return remote(
            gram_one.at[k, member], gram_one.at[k, member], one_send.at[k, other], one_recv.at[k, member],
            (r, team * group + other),
        )

    def one_wait(k, other):
        return remote(
            gram_one.at[k, other], gram_one.at[k, other], one_send.at[k, other], one_recv.at[k, other],
            (r, team * group + other),
        )

    def two_copy(k, other):
        return remote(
            gram_two.at[k, team], gram_two.at[k, team], two_send.at[k, other], two_recv.at[k, team],
            (r, other * group + member),
        )

    def two_wait(k, other):
        return remote(
            gram_two.at[k, other], gram_two.at[k, other], two_send.at[k, other], two_recv.at[k, other],
            (r, other * group + member),
        )

    def gram_start(k, value):
        gram_one[k, member] = value

        @loop(group)
        def _(other):
            @pl.when(other != member)
            def _():
                one_copy(k, other).start()

    def gram_middle(k):
        @loop(group)
        def _(other):
            @pl.when(other != member)
            def _():
                one_wait(k, other).wait_recv()

        total = gram_one[k, 0]
        for other in range(1, group):
            total = total + gram_one[k, other]
        gram_two[k, team] = total

        @loop(teams)
        def _(other):
            @pl.when(other != team)
            def _():
                two_copy(k, other).start()

    def gram_end(k):
        @loop(teams)
        def _(other):
            @pl.when(other != team)
            def _():
                two_wait(k, other).wait_recv()

        total = gram_two[k, 0]
        for other in range(1, teams):
            total = total + gram_two[k, other]
        return total

    def gather_copy(app, src, other):
        slot = c // rows
        return remote(
            src, gathered.at[app, slot], gather_send.at[app, other], gather_recv.at[app, slot], (r, other)
        )

    def gather_wait(app, i):
        return remote(
            gathered.at[app, i], gathered.at[app, i], gather_send.at[app, 0], gather_recv.at[app, i], (r, i * rows + r)
        )

    def across_copy(app, i):
        return remote(
            across_out.at[app, i], across_in.at[app, c], across_send.at[app, i], across_recv.at[app, c],
            (r, i * rows + r),
        )

    def across_wait(app, other):
        return remote(
            across_in.at[app, other], across_in.at[app, other], across_send.at[app, 0], across_recv.at[app, other],
            (r, other),
        )

    def row_copy(app, other):
        return remote(
            row_parts.at[app, r], row_parts.at[app, r], row_send.at[app, other], row_recv.at[app, r], (other, c)
        )

    def row_wait(app, other):
        return remote(
            row_parts.at[app, other], row_parts.at[app, other], row_send.at[app, other], row_recv.at[app, other],
            (other, c),
        )

    def send_block(app, src):
        @pl.when(is_owner)
        def _():
            gathered[app, c // rows] = 0.5 * src[...]

            @loop(cols, c + 1)
            def _(other):
                gather_copy(app, src, other).start()

    def send_across(app, src):
        lhs_buf[...] = stacked_split(src[...])

        @loop(slots)
        def _(i):
            block_row = i * rows + r

            @pl.when(block_row <= c)
            def _():
                if app == 0:
                    h_copy(i).wait()
                    high, low = split(h_buf[i])
                    h_high[i] = high
                    h_low[i] = low
                else:
                    high, low = h_high[i], h_low[i]
                piece = three_products(lhs_buf[...], high, low, ((1,), (1,)))

                @pl.when(block_row < c)
                def _():
                    across_out[app, i] = piece
                    across_copy(app, i).start()

                @pl.when(block_row == c)
                def _():
                    own[...] = 0.5 * piece

    def downward(app):
        acc[...] = jnp.zeros_like(acc)

        @loop(slots)
        def _(i):
            block_row = i * rows + r

            @pl.when(block_row < c)
            def _():
                gather_wait(app, i).wait_recv()

            @pl.when(block_row <= c)
            def _():
                acc[...] += three_products(
                    stacked_split(gathered[app, i]), h_high[i], h_low[i], ((1,), (0,))
                )

    def collect(app):
        @pl.when(is_owner)
        def _():
            acc[...] += own[...]

            @loop(cols, c + 1)
            def _(other):
                across_wait(app, other).wait_recv()
                acc[...] += across_in[app, other]

        row_parts[app, r] = acc[...]

        @loop(rows)
        def _(other):
            @pl.when(other != r)
            def _():
                row_copy(app, other).start()

    def row_total(app):
        @loop(rows)
        def _(other):
            @pl.when(other != r)
            def _():
                row_wait(app, other).wait_recv()

        total = row_parts[app, 0]
        for other in range(1, rows):
            total = total + row_parts[app, other]
        return total

    in_second = (lane >= vecs) & (lane < 2 * vecs)

    def first_part(matrix):
        return jnp.where(lane < vecs, matrix, 0.0)

    def second_part(matrix):
        return jnp.where(in_second, matrix, 0.0)

    def apply_first(matrix, block):
        return full_dot(first_part(matrix), placed_rows(block, 0), ((1,), (0,)))

    def apply_second(matrix, block):
        return full_dot(second_part(matrix), placed_rows(block, 1), ((1,), (0,)))

    def gram_pair(left, other):
        zero = jnp.zeros((LANES - 2 * vecs, width), F32)
        right = jnp.concatenate([left, other, zero], axis=0)
        return full_dot(left, right, ((1,), (1,))) / length

    def residual_gram(pair):
        part = second_part(pair)
        return pair - full_dot(part, placed_rows(part, 0), ((1,), (1,)))

    def record(k, pair, work, sigma):
        diagonal = pltpu.roll(pair, LANES - vecs, axis=1) + jnp.where(lane == row, sigma, 0.0)
        rec_ref[k, 0] = diagonal[:, :vecs]
        upper = jnp.where(lane >= row, first_part(work), 0.0)
        rec_ref[k, 1] = placed_rows(upper, 0).T[:vecs, :vecs]

    energy = e_ref[...]
    start = x_ref[...]
    zero_block = jnp.zeros_like(start)
    local = gram_pair(start, zero_block) + jnp.where(lane == 2 * vecs, jnp.sum(energy) / length, 0.0)

    pl.semaphore_wait(barrier, cols - 1 + rows - 1)
    send_block(0, x_ref)
    gram_start(0, local)
    send_across(0, x_ref)
    gram_middle(0)
    downward(0)
    pair = gram_end(0)
    sigma = pair[0:1, 2 * vecs : 2 * vecs + 1]
    work = factor_and_inverse(pair, row, lane, vecs)
    current = apply_second(work, start)
    collect(0)
    image = apply_second(work, row_total(0) + energy * start)
    w_buf[...] = image - sigma * current

    send_block(1, w_buf)
    shifted = w_buf[...]
    gram_start(1, gram_pair(shifted, current))
    send_across(1, w_buf)
    gram_middle(1)
    downward(1)
    pair = gram_end(1)
    work = factor_and_inverse(residual_gram(pair), row, lane, vecs)
    record(0, pair, work, sigma)
    following = apply_second(work, shifted - apply_second(pair, current))
    collect(1)
    w_image = row_total(1) + energy * shifted
    following_image = apply_second(work, w_image - apply_second(pair, image))
    last = following_image - apply_first(work, current) - sigma * following
    gram_start(2, gram_pair(last, following))
    gram_middle(2)
    pair = gram_end(2)
    work = factor_and_inverse(residual_gram(pair), row, lane, vecs)
    record(1, pair, work, sigma)
    next_ref[...] = apply_second(work, last - apply_second(pair, following))

    for app in range(ITERS):
        source = x_ref if app == 0 else w_buf

        @pl.when(is_owner)
        def _():
            @loop(cols, c + 1)
            def _(other):
                gather_copy(app, source, other).wait_send()

        @loop(slots)
        def _(i):
            @pl.when(i * rows + r < c)
            def _():
                across_copy(app, i).wait_send()

        @loop(rows)
        def _(other):
            @pl.when(other != r)
            def _():
                row_copy(app, other).wait_send()

    for k in range(ITERS + 1):
        @loop(group)
        def _(other):
            @pl.when(other != member)
            def _():
                one_copy(k, other).wait_send()

        @loop(teams)
        def _(other):
            @pl.when(other != team)
            def _():
                two_copy(k, other).wait_send()


def solution(mesh):
    rows, cols = mesh.shape["row"], mesh.shape["col"]
    group = 1
    while group * group * 4 <= cols and cols % (2 * group) == 0:
        group *= 2

    def on_device(start_block, energies, hamiltonian):
        vecs, width = start_block.shape
        slots = hamiltonian.shape[0]
        vmem = pl.BlockSpec(memory_space=pltpu.VMEM)
        dma = pltpu.SemaphoreType.DMA
        teams = cols // group
        block = (vecs, width)
        grams = ITERS + 1
        return pl.pallas_call(
            functools.partial(kernel, rows, cols, group),
            out_shape=(
                jax.ShapeDtypeStruct((ITERS, 2, vecs, vecs), F32),
                jax.ShapeDtypeStruct(block, F32),
            ),
            in_specs=[vmem, vmem, pl.BlockSpec(memory_space=pl.ANY)],
            out_specs=(vmem, vmem),
            scratch_shapes=[
                pltpu.VMEM((slots, width, width), F32),
                pltpu.VMEM((slots, width, width), BF16),
                pltpu.VMEM((slots, width, width), BF16),
                pltpu.VMEM((2 * vecs, width), BF16),
                pltpu.VMEM(block, F32),
                pltpu.VMEM((ITERS, slots) + block, F32),
                pltpu.VMEM((ITERS, slots) + block, F32),
                pltpu.VMEM((ITERS, cols) + block, F32),
                pltpu.VMEM(block, F32),
                pltpu.VMEM(block, F32),
                pltpu.VMEM((ITERS, rows) + block, F32),
                pltpu.VMEM((grams, group, vecs, LANES), F32),
                pltpu.VMEM((grams, teams, vecs, LANES), F32),
                dma((slots,)),
                dma((ITERS, cols)),
                dma((ITERS, slots)),
                dma((ITERS, slots)),
                dma((ITERS, cols)),
                dma((ITERS, rows)),
                dma((ITERS, rows)),
                dma((grams, group)),
                dma((grams, group)),
                dma((grams, teams)),
                dma((grams, teams)),
            ],
            compiler_params=pltpu.CompilerParams(
                collective_id=0, has_side_effects=True, vmem_limit_bytes=56 << 20
            ),
        )(start_block, energies.reshape(1, width), hamiltonian)

    placed = (P(None, "col"), P("col"), P("row", "col", None, None))
    return jax.shard_map(
        on_device, mesh=mesh, in_specs=placed, out_specs=(P(), P(None, "col")), check_vma=False
    )
```

```python
import functools

import jax
import jax.numpy as jnp
from jax import lax
from jax.experimental import pallas as pl
from jax.experimental.pallas import tpu as pltpu
from jax.sharding import PartitionSpec as P

ITERS = 2
LANES = 128
CORES = 2
LAG = 2
MESH = pl.DeviceIdType.MESH
F32 = jnp.float32
BF16 = jnp.bfloat16


def full_dot(left, right, contract):
    return lax.dot_general(
        left, right, (contract, ((), ())), precision=lax.Precision.HIGHEST, preferred_element_type=F32
    )


def split(value):
    high = value.astype(BF16)
    return high, (value - high.astype(F32)).astype(BF16)


def stacked_split(value):
    return jnp.concatenate(split(value), axis=0)


def three_products(stacked, high, low, contract):
    vecs = stacked.shape[0] // 2
    dims = (contract, ((), ()))
    both = lax.dot_general(stacked, high, dims, preferred_element_type=F32)
    extra = lax.dot_general(stacked[:vecs], low, dims, preferred_element_type=F32)
    return both[:vecs] + (both[vecs:] + extra)


def placed_rows(value, slot):
    vecs, width = value.shape
    parts = [jnp.zeros((vecs, width), F32)] * (LANES // vecs)
    parts[slot] = value
    return jnp.concatenate(parts, axis=0)


def factor_and_inverse(gram, row, lane, vecs):
    work = jnp.where(lane < vecs, gram, (lane - vecs == row).astype(F32))
    for step in range(vecs):
        scale = lax.rsqrt(work[step : step + 1, step : step + 1])
        pivot_row = work[step : step + 1, :] * scale
        column = work[:, step : step + 1] * scale
        work = jnp.where(
            row > step, work - column * pivot_row, jnp.where(row == step, pivot_row, work)
        )
    return work


def kernel(
    rows, cols, group,
    x_ref, e_ref, h_ref, rec_ref, next_ref,
    h_buf, h_high, h_low, lhs_buf, w_buf, gathered, across_out, across_in, pair_in, acc, own, row_parts, gram_one, gram_two,
    h_sem, gather_send, gather_recv, relay_send, pair_send, pair_recv, across_send, across_recv, row_send, row_recv, one_send, one_recv, two_send, two_recv,
):
    r, c = lax.axis_index("row"), lax.axis_index("col")
    slots = h_ref.shape[0]
    vecs, width = x_ref.shape
    length = F32(cols * width)
    member, team = c % group, c // group
    teams = cols // group
    chip, core = c // CORES, c % CORES
    chips = cols // CORES
    partner = chip * CORES + 1 - core
    is_owner = (c % rows) == r
    row = lax.broadcasted_iota(jnp.int32, (vecs, LANES), 0)
    lane = lax.broadcasted_iota(jnp.int32, (vecs, LANES), 1)

    def remote(src, dst, send, recv, where):
        return pltpu.make_async_remote_copy(
            src_ref=src, dst_ref=dst, send_sem=send, recv_sem=recv, device_id=where, device_id_type=MESH
        )

    def loop(count, start=0):
        def wrap(body):
            lax.fori_loop(start, count, lambda i, _: (body(i), 0)[1], 0)
        return wrap

    def h_copy(i):
        return pltpu.make_async_copy(h_ref.at[i, 0], h_buf.at[i], h_sem.at[i])

    barrier = pltpu.get_barrier_semaphore()

    @loop(cols)
    def _(other):
        @pl.when(other != c)
        def _():
            pl.semaphore_signal(barrier, inc=1, device_id=(r, other), device_id_type=MESH)

    @loop(rows)
    def _(other):
        @pl.when(other != r)
        def _():
            pl.semaphore_signal(barrier, inc=1, device_id=(other, c), device_id_type=MESH)

    @loop(slots)
    def _(i):
        @pl.when(i * rows + r <= c)
        def _():
            h_copy(i).start()

    def one_copy(k, other):
        return remote(
            gram_one.at[k, member], gram_one.at[k, member], one_send.at[k, other], one_recv.at[k, member],
            (r, team * group + other),
        )

    def one_wait(k, other):
        return remote(
            gram_one.at[k, other], gram_one.at[k, other], one_send.at[k, other], one_recv.at[k, other],
            (r, team * group + other),
        )

    def two_copy(k, other):
        return remote(
            gram_two.at[k, team], gram_two.at[k, team], two_send.at[k, other], two_recv.at[k, team],
            (r, other * group + member),
        )

    def two_wait(k, other):
        return remote(
            gram_two.at[k, other], gram_two.at[k, other], two_send.at[k, other], two_recv.at[k, other],
            (r, other * group + member),
        )

    def gram_start(k, value):
        gram_one[k, member] = value

        @loop(group)
        def _(other):
            @pl.when(other != member)
            def _():
                one_copy(k, other).start()

    def gram_middle(k):
        @loop(group)
        def _(other):
            @pl.when(other != member)
            def _():
                one_wait(k, other).wait_recv()

        total = gram_one[k, 0]
        for other in range(1, group):
            total = total + gram_one[k, other]
        gram_two[k, team] = total

        @loop(teams)
        def _(other):
            @pl.when(other != team)
            def _():
                two_copy(k, other).start()

    def gram_end(k):
        @loop(teams)
        def _(other):
            @pl.when(other != team)
            def _():
                two_wait(k, other).wait_recv()

        total = gram_two[k, 0]
        for other in range(1, teams):
            total = total + gram_two[k, other]
        return total

    def gather_copy(app, src, other):
        slot = c // rows
        return remote(
            src, gathered.at[app, slot], gather_send.at[app, other], gather_recv.at[app, slot], (r, other)
        )

    def gather_wait(app, i):
        return remote(
            gathered.at[app, i], gathered.at[app, i], gather_send.at[app, 0], gather_recv.at[app, i], (r, i * rows + r)
        )

    def relay_copy(app, i):
        return remote(
            gathered.at[app, i], gathered.at[app, i], relay_send.at[app, i], gather_recv.at[app, i], (r, partner)
        )

    def pair_copy(app, i):
        return remote(
            across_out.at[app, i], pair_in.at[app, i], pair_send.at[app, i], pair_recv.at[app, i], (r, partner)
        )

    def across_copy(app, i):
        return remote(
            across_out.at[app, i], across_in.at[app, chip], across_send.at[app, i], across_recv.at[app, chip],
            (r, i * rows + r),
        )

    def across_wait(app, other):
        return remote(
            across_in.at[app, other], across_in.at[app, other], across_send.at[app, 0], across_recv.at[app, other],
            (r, partner),
        )

    def leaves_chip(i):
        return (i * rows + r) // CORES < chip

    def is_relayed(i):
        return leaves_chip(i) & ((i * rows + r) % CORES == core)

    def goes_to_partner(i):
        return leaves_chip(i) & (i % CORES != core)

    def is_finished_here(i):
        return leaves_chip(i) & (i % CORES == core)

    def stays_on_chip(i):
        return (i * rows + r < c) & ((i * rows + r) // CORES == chip)

    def row_copy(app, other):
        return remote(
            row_parts.at[app, r], row_parts.at[app, r], row_send.at[app, other], row_recv.at[app, r], (other, c)
        )

    def row_wait(app, other):
        return remote(
            row_parts.at[app, other], row_parts.at[app, other], row_send.at[app, other], row_recv.at[app, other],
            (other, c),
        )

    def targets(body):
        @pl.when(is_owner)
        def _():
            @loop(chips - 1 - chip)
            def _(step):
                body((chips - 1 - step) * CORES + core)

            @pl.when(core == 0)
            def _():
                body(partner)

    def send_block(app, src):
        @pl.when(is_owner)
        def _():
            gathered[app, c // rows] = 0.5 * src[...]

        targets(lambda other: gather_copy(app, src, other).start())

    def split_blocks():
        @loop(slots)
        def _(i):
            @pl.when(i * rows + r <= c)
            def _():
                h_copy(i).wait()
                high, low = split(h_buf[i])
                h_high[i] = high
                h_low[i] = low

    def send_across(app, src):
        lhs_buf[...] = stacked_split(src[...])

        def finish(i):
            @pl.when(is_finished_here(i))
            def _():
                pair_copy(app, i).wait_recv()
                across_out[app, i] += pair_in[app, i]
                across_copy(app, i).start()

        @loop(slots)
        def _(i):
            block_row = i * rows + r

            @pl.when(block_row <= c)
            def _():
                piece = three_products(lhs_buf[...], h_high[i], h_low[i], ((1,), (1,)))

                @pl.when(block_row < c)
                def _():
                    across_out[app, i] = piece

                @pl.when(goes_to_partner(i))
                def _():
                    pair_copy(app, i).start()

                @pl.when(stays_on_chip(i))
                def _():
                    across_copy(app, i).start()

                @pl.when(block_row == c)
                def _():
                    own[...] = 0.5 * piece

            @pl.when(i >= LAG)
            def _():
                finish(i - LAG)

        for step in range(min(LAG, slots)):
            finish(slots - min(LAG, slots) + step)

    def downward(app):
        acc[...] = jnp.zeros_like(acc)

        @loop(slots)
        def _(step):
            i = slots - 1 - step
            block_row = i * rows + r

            @pl.when(block_row < c)
            def _():
                gather_wait(app, i).wait_recv()

            @pl.when(is_relayed(i))
            def _():
                relay_copy(app, i).start()

            @pl.when(block_row <= c)
            def _():
                acc[...] += three_products(
                    stacked_split(gathered[app, i]), h_high[i], h_low[i], ((1,), (0,))
                )

    def collect(app):
        @pl.when(is_owner)
        def _():
            acc[...] += own[...]

            @loop(chips, chip + core)
            def _(other):
                across_wait(app, other).wait_recv()
                acc[...] += across_in[app, other]

        row_parts[app, r] = acc[...]

        @loop(rows)
        def _(other):
            @pl.when(other != r)
            def _():
                row_copy(app, other).start()

    def row_total(app):
        @loop(rows)
        def _(other):
            @pl.when(other != r)
            def _():
                row_wait(app, other).wait_recv()

        total = row_parts[app, 0]
        for other in range(1, rows):
            total = total + row_parts[app, other]
        return total

    in_second = (lane >= vecs) & (lane < 2 * vecs)

    def first_part(matrix):
        return jnp.where(lane < vecs, matrix, 0.0)

    def second_part(matrix):
        return jnp.where(in_second, matrix, 0.0)

    def apply_first(matrix, block):
        return full_dot(first_part(matrix), placed_rows(block, 0), ((1,), (0,)))

    def apply_second(matrix, block):
        return full_dot(second_part(matrix), placed_rows(block, 1), ((1,), (0,)))

    def gram_pair(left, other):
        zero = jnp.zeros((LANES - 2 * vecs, width), F32)
        right = jnp.concatenate([left, other, zero], axis=0)
        return full_dot(left, right, ((1,), (1,))) / length

    def residual_gram(pair):
        part = second_part(pair)
        return pair - full_dot(part, placed_rows(part, 0), ((1,), (1,)))

    def record(k, pair, work, sigma):
        diagonal = pltpu.roll(pair, LANES - vecs, axis=1) + jnp.where(lane == row, sigma, 0.0)
        rec_ref[k, 0] = diagonal[:, :vecs]
        upper = jnp.where(lane >= row, first_part(work), 0.0)
        rec_ref[k, 1] = placed_rows(upper, 0).T[:vecs, :vecs]

    energy = e_ref[...]
    start = x_ref[...]
    zero_block = jnp.zeros_like(start)
    local = gram_pair(start, zero_block) + jnp.where(lane == 2 * vecs, jnp.sum(energy) / length, 0.0)

    split_blocks()
    pl.semaphore_wait(barrier, cols - 1 + rows - 1)
    send_block(0, x_ref)
    gram_start(0, local)
    send_across(0, x_ref)
    gram_middle(0)
    downward(0)
    pair = gram_end(0)
    sigma = pair[0:1, 2 * vecs : 2 * vecs + 1]
    work = factor_and_inverse(pair, row, lane, vecs)
    current = apply_second(work, start)
    collect(0)
    image = apply_second(work, row_total(0) + energy * start)
    w_buf[...] = image - sigma * current

    send_block(1, w_buf)
    shifted = w_buf[...]
    gram_start(1, gram_pair(shifted, current))
    send_across(1, w_buf)
    gram_middle(1)
    downward(1)
    pair = gram_end(1)
    work = factor_and_inverse(residual_gram(pair), row, lane, vecs)
    record(0, pair, work, sigma)
    following = apply_second(work, shifted - apply_second(pair, current))
    collect(1)
    w_image = row_total(1) + energy * shifted
    following_image = apply_second(work, w_image - apply_second(pair, image))
    last = following_image - apply_first(work, current) - sigma * following
    gram_start(2, gram_pair(last, following))
    gram_middle(2)
    pair = gram_end(2)
    work = factor_and_inverse(residual_gram(pair), row, lane, vecs)
    record(1, pair, work, sigma)
    next_ref[...] = apply_second(work, last - apply_second(pair, following))

    for app in range(ITERS):
        source = x_ref if app == 0 else w_buf

        targets(lambda other: gather_copy(app, source, other).wait_send())

        @loop(slots)
        def _(i):
            @pl.when(is_relayed(i))
            def _():
                relay_copy(app, i).wait_send()

            @pl.when(goes_to_partner(i))
            def _():
                pair_copy(app, i).wait_send()

            @pl.when(is_finished_here(i) | stays_on_chip(i))
            def _():
                across_copy(app, i).wait_send()

        @loop(rows)
        def _(other):
            @pl.when(other != r)
            def _():
                row_copy(app, other).wait_send()

    for k in range(ITERS + 1):
        @loop(group)
        def _(other):
            @pl.when(other != member)
            def _():
                one_copy(k, other).wait_send()

        @loop(teams)
        def _(other):
            @pl.when(other != team)
            def _():
                two_copy(k, other).wait_send()


def solution(mesh):
    rows, cols = mesh.shape["row"], mesh.shape["col"]
    group = 1
    while group * group * 4 <= cols and cols % (2 * group) == 0:
        group *= 2

    def on_device(start_block, energies, hamiltonian):
        vecs, width = start_block.shape
        slots = hamiltonian.shape[0]
        vmem = pl.BlockSpec(memory_space=pltpu.VMEM)
        dma = pltpu.SemaphoreType.DMA
        teams = cols // group
        block = (vecs, width)
        grams = ITERS + 1
        return pl.pallas_call(
            functools.partial(kernel, rows, cols, group),
            out_shape=(
                jax.ShapeDtypeStruct((ITERS, 2, vecs, vecs), F32),
                jax.ShapeDtypeStruct(block, F32),
            ),
            in_specs=[vmem, vmem, pl.BlockSpec(memory_space=pl.ANY)],
            out_specs=(vmem, vmem),
            scratch_shapes=[
                pltpu.VMEM((slots, width, width), F32),
                pltpu.VMEM((slots, width, width), BF16),
                pltpu.VMEM((slots, width, width), BF16),
                pltpu.VMEM((2 * vecs, width), BF16),
                pltpu.VMEM(block, F32),
                pltpu.VMEM((ITERS, slots) + block, F32),
                pltpu.VMEM((ITERS, slots) + block, F32),
                pltpu.VMEM((ITERS, cols // CORES) + block, F32),
                pltpu.VMEM((ITERS, slots) + block, F32),
                pltpu.VMEM(block, F32),
                pltpu.VMEM(block, F32),
                pltpu.VMEM((ITERS, rows) + block, F32),
                pltpu.VMEM((grams, group, vecs, LANES), F32),
                pltpu.VMEM((grams, teams, vecs, LANES), F32),
                dma((slots,)),
                dma((ITERS, cols)),
                dma((ITERS, slots)),
                dma((ITERS, slots)),
                dma((ITERS, slots)),
                dma((ITERS, slots)),
                dma((ITERS, slots)),
                dma((ITERS, cols // CORES)),
                dma((ITERS, rows)),
                dma((ITERS, rows)),
                dma((grams, group)),
                dma((grams, group)),
                dma((grams, teams)),
                dma((grams, teams)),
            ],
            compiler_params=pltpu.CompilerParams(
                collective_id=0, has_side_effects=True, vmem_limit_bytes=56 << 20
            ),
        )(start_block, energies.reshape(1, width), hamiltonian)

    placed = (P(None, "col"), P("col"), P("row", "col", None, None))
    return jax.shard_map(
        on_device, mesh=mesh, in_specs=placed, out_specs=(P(), P(None, "col")), check_vma=False
    )
```

```python
import functools

import jax
import jax.numpy as jnp
from jax import lax
from jax.experimental import pallas as pl
from jax.experimental.pallas import tpu as pltpu
from jax.sharding import PartitionSpec as P

ITERS = 2
LANES = 128
CORES = 2
LAG = 2
MESH = pl.DeviceIdType.MESH
F32 = jnp.float32
BF16 = jnp.bfloat16


def full_dot(left, right, contract):
    return lax.dot_general(
        left, right, (contract, ((), ())), precision=lax.Precision.HIGHEST, preferred_element_type=F32
    )


def split(value):
    high = value.astype(BF16)
    return high, (value - high.astype(F32)).astype(BF16)


def stacked_split(value):
    return jnp.concatenate(split(value), axis=0)


def three_products(stacked, high, low, contract):
    vecs = stacked.shape[0] // 2
    dims = (contract, ((), ()))
    both = lax.dot_general(stacked, high, dims, preferred_element_type=F32)
    extra = lax.dot_general(stacked[:vecs], low, dims, preferred_element_type=F32)
    return both[:vecs] + (both[vecs:] + extra)


def placed_rows(value, slot):
    vecs, width = value.shape
    parts = [jnp.zeros((vecs, width), F32)] * (LANES // vecs)
    parts[slot] = value
    return jnp.concatenate(parts, axis=0)


def factor_and_inverse(gram, row, lane, vecs):
    work = jnp.where(lane < vecs, gram, (lane - vecs == row).astype(F32))
    for step in range(0, vecs, 2):
        top, low = work[step : step + 1, :], work[step + 1 : step + 2, :]
        left, right = work[:, step : step + 1], work[:, step + 1 : step + 2]
        first, cross = top[:, step : step + 1], top[:, step + 1 : step + 2]
        second = low[:, step + 1 : step + 2]
        inverse = 1.0 / first
        ratio = cross * inverse
        low = low - ratio * top
        right = right - ratio * left
        reduced = work - left * (top * inverse) - right * (low * (1.0 / (second - cross * ratio)))
        work = jnp.where(row > step + 1, reduced, jnp.where(row == step + 1, low, work))
    pivots = jnp.sum(jnp.where(lane == row, work, 0.0), axis=1, keepdims=True)
    return work * lax.rsqrt(pivots)


def kernel(
    rows, cols, group,
    x_ref, e_ref, h_ref, rec_ref, next_ref,
    h_buf, h_high, h_low, lhs_buf, w_buf, gathered, across_out, across_in, pair_in, acc, own, row_parts, gram_one, gram_two,
    h_sem, gather_send, gather_recv, relay_send, pair_send, pair_recv, across_send, across_recv, row_send, row_recv, one_send, one_recv, two_send, two_recv,
):
    r, c = lax.axis_index("row"), lax.axis_index("col")
    slots = h_ref.shape[0]
    vecs, width = x_ref.shape
    length = F32(cols * width)
    member, team = c % group, c // group
    teams = cols // group
    chip, core = c // CORES, c % CORES
    chips = cols // CORES
    partner = chip * CORES + 1 - core
    is_owner = (c % rows) == r
    row = lax.broadcasted_iota(jnp.int32, (vecs, LANES), 0)
    lane = lax.broadcasted_iota(jnp.int32, (vecs, LANES), 1)

    def remote(src, dst, send, recv, where):
        return pltpu.make_async_remote_copy(
            src_ref=src, dst_ref=dst, send_sem=send, recv_sem=recv, device_id=where, device_id_type=MESH
        )

    def loop(count, start=0):
        def wrap(body):
            lax.fori_loop(start, count, lambda i, _: (body(i), 0)[1], 0)
        return wrap

    def h_copy(i):
        return pltpu.make_async_copy(h_ref.at[i, 0], h_buf.at[i], h_sem.at[i])

    barrier = pltpu.get_barrier_semaphore()

    @loop(cols)
    def _(other):
        @pl.when(other != c)
        def _():
            pl.semaphore_signal(barrier, inc=1, device_id=(r, other), device_id_type=MESH)

    @loop(rows)
    def _(other):
        @pl.when(other != r)
        def _():
            pl.semaphore_signal(barrier, inc=1, device_id=(other, c), device_id_type=MESH)

    @loop(slots)
    def _(i):
        @pl.when(i * rows + r <= c)
        def _():
            h_copy(i).start()

    def one_copy(k, other):
        return remote(
            gram_one.at[k, member], gram_one.at[k, member], one_send.at[k, other], one_recv.at[k, member],
            (r, team * group + other),
        )

    def one_wait(k, other):
        return remote(
            gram_one.at[k, other], gram_one.at[k, other], one_send.at[k, other], one_recv.at[k, other],
            (r, team * group + other),
        )

    def two_copy(k, other):
        return remote(
            gram_two.at[k, team], gram_two.at[k, team], two_send.at[k, other], two_recv.at[k, team],
            (r, other * group + member),
        )

    def two_wait(k, other):
        return remote(
            gram_two.at[k, other], gram_two.at[k, other], two_send.at[k, other], two_recv.at[k, other],
            (r, other * group + member),
        )

    def gram_start(k, value):
        gram_one[k, member] = value

        @loop(group)
        def _(other):
            @pl.when(other != member)
            def _():
                one_copy(k, other).start()

    def gram_middle(k):
        @loop(group)
        def _(other):
            @pl.when(other != member)
            def _():
                one_wait(k, other).wait_recv()

        total = gram_one[k, 0]
        for other in range(1, group):
            total = total + gram_one[k, other]
        gram_two[k, team] = total

        @loop(teams)
        def _(other):
            @pl.when(other != team)
            def _():
                two_copy(k, other).start()

    def gram_end(k):
        @loop(teams)
        def _(other):
            @pl.when(other != team)
            def _():
                two_wait(k, other).wait_recv()

        total = gram_two[k, 0]
        for other in range(1, teams):
            total = total + gram_two[k, other]
        return total

    def gather_copy(app, src, other):
        slot = c // rows
        return remote(
            src, gathered.at[app, slot], gather_send.at[app, other], gather_recv.at[app, slot], (r, other)
        )

    def gather_wait(app, i):
        return remote(
            gathered.at[app, i], gathered.at[app, i], gather_send.at[app, 0], gather_recv.at[app, i], (r, i * rows + r)
        )

    def relay_copy(app, i):
        return remote(
            gathered.at[app, i], gathered.at[app, i], relay_send.at[app, i], gather_recv.at[app, i], (r, partner)
        )

    def pair_copy(app, i):
        return remote(
            across_out.at[app, i], pair_in.at[app, i], pair_send.at[app, i], pair_recv.at[app, i], (r, partner)
        )

    def across_copy(app, i):
        return remote(
            across_out.at[app, i], across_in.at[app, chip], across_send.at[app, i], across_recv.at[app, chip],
            (r, i * rows + r),
        )

    def across_wait(app, other):
        return remote(
            across_in.at[app, other], across_in.at[app, other], across_send.at[app, 0], across_recv.at[app, other],
            (r, partner),
        )

    def leaves_chip(i):
        return (i * rows + r) // CORES < chip

    def is_relayed(i):
        return leaves_chip(i) & ((i * rows + r) % CORES == core)

    def goes_to_partner(i):
        return leaves_chip(i) & (i % CORES != core)

    def is_finished_here(i):
        return leaves_chip(i) & (i % CORES == core)

    def stays_on_chip(i):
        return (i * rows + r < c) & ((i * rows + r) // CORES == chip)

    def row_copy(app, other):
        return remote(
            row_parts.at[app, r], row_parts.at[app, r], row_send.at[app, other], row_recv.at[app, r], (other, c)
        )

    def row_wait(app, other):
        return remote(
            row_parts.at[app, other], row_parts.at[app, other], row_send.at[app, other], row_recv.at[app, other],
            (other, c),
        )

    def targets(body):
        @pl.when(is_owner)
        def _():
            @loop(chips - 1 - chip)
            def _(step):
                body((chips - 1 - step) * CORES + core)

            @pl.when(core == 0)
            def _():
                body(partner)

    def send_block(app, src):
        @pl.when(is_owner)
        def _():
            gathered[app, c // rows] = 0.5 * src[...]

        targets(lambda other: gather_copy(app, src, other).start())

    def split_blocks():
        @loop(slots)
        def _(i):
            @pl.when(i * rows + r <= c)
            def _():
                h_copy(i).wait()
                high, low = split(h_buf[i])
                h_high[i] = high
                h_low[i] = low

    def send_across(app, src):
        lhs_buf[...] = stacked_split(src[...])

        def finish(i):
            @pl.when(is_finished_here(i))
            def _():
                pair_copy(app, i).wait_recv()
                across_out[app, i] += pair_in[app, i]
                across_copy(app, i).start()

        @loop(slots)
        def _(i):
            block_row = i * rows + r

            @pl.when(block_row <= c)
            def _():
                piece = three_products(lhs_buf[...], h_high[i], h_low[i], ((1,), (1,)))

                @pl.when(block_row < c)
                def _():
                    across_out[app, i] = piece

                @pl.when(goes_to_partner(i))
                def _():
                    pair_copy(app, i).start()

                @pl.when(stays_on_chip(i))
                def _():
                    across_copy(app, i).start()

                @pl.when(block_row == c)
                def _():
                    own[...] = 0.5 * piece

            @pl.when(i >= LAG)
            def _():
                finish(i - LAG)

        for step in range(min(LAG, slots)):
            finish(slots - min(LAG, slots) + step)

    def downward(app):
        acc[...] = jnp.zeros_like(acc)

        @loop(slots)
        def _(step):
            i = slots - 1 - step
            block_row = i * rows + r

            @pl.when(block_row < c)
            def _():
                gather_wait(app, i).wait_recv()

            @pl.when(is_relayed(i))
            def _():
                relay_copy(app, i).start()

            @pl.when(block_row <= c)
            def _():
                acc[...] += three_products(
                    stacked_split(gathered[app, i]), h_high[i], h_low[i], ((1,), (0,))
                )

    def collect(app):
        @pl.when(is_owner)
        def _():
            acc[...] += own[...]

            @loop(chips, chip + core)
            def _(other):
                across_wait(app, other).wait_recv()
                acc[...] += across_in[app, other]

        row_parts[app, r] = acc[...]

        @loop(rows)
        def _(other):
            @pl.when(other != r)
            def _():
                row_copy(app, other).start()

    def row_total(app):
        @loop(rows)
        def _(other):
            @pl.when(other != r)
            def _():
                row_wait(app, other).wait_recv()

        total = row_parts[app, 0]
        for other in range(1, rows):
            total = total + row_parts[app, other]
        return total

    in_second = (lane >= vecs) & (lane < 2 * vecs)

    def first_part(matrix):
        return jnp.where(lane < vecs, matrix, 0.0)

    def second_part(matrix):
        return jnp.where(in_second, matrix, 0.0)

    def apply_first(matrix, block):
        return full_dot(first_part(matrix), placed_rows(block, 0), ((1,), (0,)))

    def apply_second(matrix, block):
        return full_dot(second_part(matrix), placed_rows(block, 1), ((1,), (0,)))

    def gram_pair(left, other):
        zero = jnp.zeros((LANES - 2 * vecs, width), F32)
        right = jnp.concatenate([left, other, zero], axis=0)
        return full_dot(left, right, ((1,), (1,))) / length

    def residual_gram(pair):
        part = second_part(pair)
        return pair - full_dot(part, placed_rows(part, 0), ((1,), (1,)))

    def record(k, pair, work, sigma):
        diagonal = pltpu.roll(pair, LANES - vecs, axis=1) + jnp.where(lane == row, sigma, 0.0)
        rec_ref[k, 0] = diagonal[:, :vecs]
        upper = jnp.where(lane >= row, first_part(work), 0.0)
        rec_ref[k, 1] = placed_rows(upper, 0).T[:vecs, :vecs]

    energy = e_ref[...]
    start = x_ref[...]
    zero_block = jnp.zeros_like(start)
    local = gram_pair(start, zero_block) + jnp.where(lane == 2 * vecs, jnp.sum(energy) / length, 0.0)

    split_blocks()
    pl.semaphore_wait(barrier, cols - 1 + rows - 1)
    send_block(0, x_ref)
    gram_start(0, local)
    send_across(0, x_ref)
    gram_middle(0)
    downward(0)
    collect(0)
    pair = gram_end(0)
    sigma = pair[0:1, 2 * vecs : 2 * vecs + 1]
    work = factor_and_inverse(pair, row, lane, vecs)
    current = apply_second(work, start)
    image = apply_second(work, row_total(0) + energy * start)
    w_buf[...] = image - sigma * current

    send_block(1, w_buf)
    shifted = w_buf[...]
    gram_start(1, gram_pair(shifted, current))
    send_across(1, w_buf)
    gram_middle(1)
    downward(1)
    collect(1)
    pair = gram_end(1)
    work = factor_and_inverse(residual_gram(pair), row, lane, vecs)
    record(0, pair, work, sigma)
    following = apply_second(work, shifted - apply_second(pair, current))
    w_image = row_total(1) + energy * shifted
    following_image = apply_second(work, w_image - apply_second(pair, image))
    last = following_image - apply_first(work, current) - sigma * following
    gram_start(2, gram_pair(last, following))
    gram_middle(2)
    pair = gram_end(2)
    work = factor_and_inverse(residual_gram(pair), row, lane, vecs)
    record(1, pair, work, sigma)
    next_ref[...] = apply_second(work, last - apply_second(pair, following))

    for app in range(ITERS):
        source = x_ref if app == 0 else w_buf

        targets(lambda other: gather_copy(app, source, other).wait_send())

        @loop(slots)
        def _(i):
            @pl.when(is_relayed(i))
            def _():
                relay_copy(app, i).wait_send()

            @pl.when(goes_to_partner(i))
            def _():
                pair_copy(app, i).wait_send()

            @pl.when(is_finished_here(i) | stays_on_chip(i))
            def _():
                across_copy(app, i).wait_send()

        @loop(rows)
        def _(other):
            @pl.when(other != r)
            def _():
                row_copy(app, other).wait_send()

    for k in range(ITERS + 1):
        @loop(group)
        def _(other):
            @pl.when(other != member)
            def _():
                one_copy(k, other).wait_send()

        @loop(teams)
        def _(other):
            @pl.when(other != team)
            def _():
                two_copy(k, other).wait_send()


def solution(mesh):
    rows, cols = mesh.shape["row"], mesh.shape["col"]
    group = 1
    while group * group * 4 <= cols and cols % (2 * group) == 0:
        group *= 2

    def on_device(start_block, energies, hamiltonian):
        vecs, width = start_block.shape
        slots = hamiltonian.shape[0]
        vmem = pl.BlockSpec(memory_space=pltpu.VMEM)
        dma = pltpu.SemaphoreType.DMA
        teams = cols // group
        block = (vecs, width)
        grams = ITERS + 1
        return pl.pallas_call(
            functools.partial(kernel, rows, cols, group),
            out_shape=(
                jax.ShapeDtypeStruct((ITERS, 2, vecs, vecs), F32),
                jax.ShapeDtypeStruct(block, F32),
            ),
            in_specs=[vmem, vmem, pl.BlockSpec(memory_space=pl.ANY)],
            out_specs=(vmem, vmem),
            scratch_shapes=[
                pltpu.VMEM((slots, width, width), F32),
                pltpu.VMEM((slots, width, width), BF16),
                pltpu.VMEM((slots, width, width), BF16),
                pltpu.VMEM((2 * vecs, width), BF16),
                pltpu.VMEM(block, F32),
                pltpu.VMEM((ITERS, slots) + block, F32),
                pltpu.VMEM((ITERS, slots) + block, F32),
                pltpu.VMEM((ITERS, cols // CORES) + block, F32),
                pltpu.VMEM((ITERS, slots) + block, F32),
                pltpu.VMEM(block, F32),
                pltpu.VMEM(block, F32),
                pltpu.VMEM((ITERS, rows) + block, F32),
                pltpu.VMEM((grams, group, vecs, LANES), F32),
                pltpu.VMEM((grams, teams, vecs, LANES), F32),
                dma((slots,)),
                dma((ITERS, cols)),
                dma((ITERS, slots)),
                dma((ITERS, slots)),
                dma((ITERS, slots)),
                dma((ITERS, slots)),
                dma((ITERS, slots)),
                dma((ITERS, cols // CORES)),
                dma((ITERS, rows)),
                dma((ITERS, rows)),
                dma((grams, group)),
                dma((grams, group)),
                dma((grams, teams)),
                dma((grams, teams)),
            ],
            compiler_params=pltpu.CompilerParams(
                collective_id=0, has_side_effects=True, vmem_limit_bytes=56 << 20
            ),
        )(start_block, energies.reshape(1, width), hamiltonian)

    placed = (P(None, "col"), P("col"), P("row", "col", None, None))
    return jax.shard_map(
        on_device, mesh=mesh, in_specs=placed, out_specs=(P(), P(None, "col")), check_vma=False
    )
```

```python
import functools

import jax
import jax.numpy as jnp
from jax import lax
from jax.experimental import pallas as pl
from jax.experimental.pallas import tpu as pltpu
from jax.sharding import PartitionSpec as P

ITERS = 2
LANES = 128
CORES = 2
LAG = 2
MESH = pl.DeviceIdType.MESH
F32 = jnp.float32
BF16 = jnp.bfloat16


def full_dot(left, right, contract):
    return lax.dot_general(
        left, right, (contract, ((), ())), precision=lax.Precision.HIGHEST, preferred_element_type=F32
    )


def split(value):
    high = value.astype(BF16)
    return high, (value - high.astype(F32)).astype(BF16)


def stacked_split(value):
    return jnp.concatenate(split(value), axis=0)


def three_products(stacked, high, low, contract):
    vecs = stacked.shape[0] // 2
    dims = (contract, ((), ()))
    both = lax.dot_general(stacked, high, dims, preferred_element_type=F32)
    extra = lax.dot_general(stacked[:vecs], low, dims, preferred_element_type=F32)
    return both[:vecs] + (both[vecs:] + extra)


def placed_rows(value, slot):
    vecs, width = value.shape
    parts = [jnp.zeros((vecs, width), F32)] * (LANES // vecs)
    parts[slot] = value
    return jnp.concatenate(parts, axis=0)


def factor_and_inverse(gram, row, lane, vecs):
    work = jnp.where(lane < vecs, gram, (lane - vecs == row).astype(F32))
    for step in range(0, vecs, 2):
        top, low = work[step : step + 1, :], work[step + 1 : step + 2, :]
        left, right = work[:, step : step + 1], work[:, step + 1 : step + 2]
        first, cross = top[:, step : step + 1], top[:, step + 1 : step + 2]
        second = low[:, step + 1 : step + 2]
        inverse = 1.0 / first
        ratio = cross * inverse
        low = low - ratio * top
        right = right - ratio * left
        reduced = work - left * (top * inverse) - right * (low * (1.0 / (second - cross * ratio)))
        work = jnp.where(row > step + 1, reduced, jnp.where(row == step + 1, low, work))
    pivots = jnp.sum(jnp.where(lane == row, work, 0.0), axis=1, keepdims=True)
    return work * lax.rsqrt(pivots)


def kernel(
    rows, cols, group,
    x_ref, e_ref, h_ref, rec_ref, next_ref,
    h_buf, h_high, h_low, lhs_buf, w_buf, gathered, across_out, across_in, pair_in, acc, own, row_parts, gram_one, gram_two,
    h_sem, gather_send, gather_recv, relay_send, pair_send, pair_recv, across_send, across_recv, row_send, row_recv, one_send, one_recv, two_send, two_recv,
):
    r, c = lax.axis_index("row"), lax.axis_index("col")
    slots = h_ref.shape[0]
    vecs, width = x_ref.shape
    length = F32(cols * width)
    member, team = c % group, c // group
    teams = cols // group
    chip, core = c // CORES, c % CORES
    chips = cols // CORES
    partner = chip * CORES + 1 - core
    is_owner = (c % rows) == r
    row = lax.broadcasted_iota(jnp.int32, (vecs, LANES), 0)
    lane = lax.broadcasted_iota(jnp.int32, (vecs, LANES), 1)

    def remote(src, dst, send, recv, where):
        return pltpu.make_async_remote_copy(
            src_ref=src, dst_ref=dst, send_sem=send, recv_sem=recv, device_id=where, device_id_type=MESH
        )

    def loop(count, start=0):
        def wrap(body):
            lax.fori_loop(start, count, lambda i, _: (body(i), 0)[1], 0)
        return wrap

    def h_copy(i):
        return pltpu.make_async_copy(h_ref.at[i, 0], h_buf.at[i], h_sem.at[i])

    barrier = pltpu.get_barrier_semaphore()

    @loop(cols)
    def _(other):
        @pl.when(other != c)
        def _():
            pl.semaphore_signal(barrier, inc=1, device_id=(r, other), device_id_type=MESH)

    @loop(rows)
    def _(other):
        @pl.when(other != r)
        def _():
            pl.semaphore_signal(barrier, inc=1, device_id=(other, c), device_id_type=MESH)

    @loop(slots)
    def _(i):
        @pl.when(i * rows + r <= c)
        def _():
            h_copy(i).start()

    def one_copy(k, other):
        return remote(
            gram_one.at[k, member], gram_one.at[k, member], one_send.at[k, other], one_recv.at[k, member],
            (r, team * group + other),
        )

    def one_wait(k, other):
        return remote(
            gram_one.at[k, other], gram_one.at[k, other], one_send.at[k, other], one_recv.at[k, other],
            (r, team * group + other),
        )

    def two_copy(k, other):
        return remote(
            gram_two.at[k, team], gram_two.at[k, team], two_send.at[k, other], two_recv.at[k, team],
            (r, other * group + member),
        )

    def two_wait(k, other):
        return remote(
            gram_two.at[k, other], gram_two.at[k, other], two_send.at[k, other], two_recv.at[k, other],
            (r, other * group + member),
        )

    def gram_start(k, value):
        gram_one[k, member] = value

        @loop(group)
        def _(other):
            @pl.when(other != member)
            def _():
                one_copy(k, other).start()

    def gram_middle(k):
        @loop(group)
        def _(other):
            @pl.when(other != member)
            def _():
                one_wait(k, other).wait_recv()

        total = gram_one[k, 0]
        for other in range(1, group):
            total = total + gram_one[k, other]
        gram_two[k, team] = total

        @loop(teams)
        def _(other):
            @pl.when(other != team)
            def _():
                two_copy(k, other).start()

    def gram_end(k):
        @loop(teams)
        def _(other):
            @pl.when(other != team)
            def _():
                two_wait(k, other).wait_recv()

        total = gram_two[k, 0]
        for other in range(1, teams):
            total = total + gram_two[k, other]
        return total

    def gather_copy(app, src, other):
        slot = c // rows
        return remote(
            src, gathered.at[app, slot], gather_send.at[app, other], gather_recv.at[app, slot], (r, other)
        )

    def gather_wait(app, i):
        return remote(
            gathered.at[app, i], gathered.at[app, i], gather_send.at[app, 0], gather_recv.at[app, i], (r, i * rows + r)
        )

    def relay_copy(app, i):
        return remote(
            gathered.at[app, i], gathered.at[app, i], relay_send.at[app, i], gather_recv.at[app, i], (r, partner)
        )

    def pair_copy(app, i):
        return remote(
            across_out.at[app, i], pair_in.at[app, i], pair_send.at[app, i], pair_recv.at[app, i], (r, partner)
        )

    def across_copy(app, i):
        return remote(
            across_out.at[app, i], across_in.at[app, chip], across_send.at[app, i], across_recv.at[app, chip],
            (r, i * rows + r),
        )

    def across_wait(app, other):
        return remote(
            across_in.at[app, other], across_in.at[app, other], across_send.at[app, 0], across_recv.at[app, other],
            (r, partner),
        )

    def leaves_chip(i):
        return (i * rows + r) // CORES < chip

    def is_relayed(i):
        return leaves_chip(i) & ((i * rows + r) % CORES == core)

    def goes_to_partner(i):
        return leaves_chip(i) & (i % CORES != core)

    def is_finished_here(i):
        return leaves_chip(i) & (i % CORES == core)

    def stays_on_chip(i):
        return (i * rows + r < c) & ((i * rows + r) // CORES == chip)

    def row_copy(app, other):
        return remote(
            row_parts.at[app, r], row_parts.at[app, r], row_send.at[app, other], row_recv.at[app, r], (other, c)
        )

    def row_wait(app, other):
        return remote(
            row_parts.at[app, other], row_parts.at[app, other], row_send.at[app, other], row_recv.at[app, other],
            (other, c),
        )

    def targets(body):
        @pl.when(is_owner)
        def _():
            @loop(chips - 1 - chip)
            def _(step):
                body((chips - 1 - step) * CORES + core)

            @pl.when(core == 0)
            def _():
                body(partner)

    def send_block(app, src):
        @pl.when(is_owner)
        def _():
            gathered[app, c // rows] = 0.5 * src[...]

        targets(lambda other: gather_copy(app, src, other).start())

    def split_blocks():
        @loop(slots)
        def _(i):
            @pl.when(i * rows + r <= c)
            def _():
                h_copy(i).wait()
                high, low = split(h_buf[i])
                h_high[i] = high
                h_low[i] = low

    def send_across(app, src):
        lhs_buf[...] = stacked_split(src[...])

        def finish(i):
            @pl.when(is_finished_here(i))
            def _():
                pair_copy(app, i).wait_recv()
                across_out[app, i] += pair_in[app, i]
                across_copy(app, i).start()

        @loop(slots)
        def _(i):
            block_row = i * rows + r

            @pl.when(block_row <= c)
            def _():
                piece = three_products(lhs_buf[...], h_high[i], h_low[i], ((1,), (1,)))

                @pl.when(block_row < c)
                def _():
                    across_out[app, i] = piece

                @pl.when(goes_to_partner(i))
                def _():
                    pair_copy(app, i).start()

                @pl.when(stays_on_chip(i))
                def _():
                    across_copy(app, i).start()

                @pl.when(block_row == c)
                def _():
                    own[...] = 0.5 * piece

            @pl.when(i >= LAG)
            def _():
                finish(i - LAG)

        for step in range(min(LAG, slots)):
            finish(slots - min(LAG, slots) + step)

    def downward(app):
        acc[...] = jnp.zeros_like(acc)

        @loop(slots)
        def _(step):
            i = slots - 1 - step
            block_row = i * rows + r

            @pl.when(block_row < c)
            def _():
                gather_wait(app, i).wait_recv()

            @pl.when(is_relayed(i))
            def _():
                relay_copy(app, i).start()

            @pl.when(block_row <= c)
            def _():
                acc[...] += three_products(
                    stacked_split(gathered[app, i]), h_high[i], h_low[i], ((1,), (0,))
                )

    def collect(app):
        @pl.when(is_owner)
        def _():
            acc[...] += own[...]

            @loop(chips, chip + core)
            def _(other):
                across_wait(app, other).wait_recv()
                acc[...] += across_in[app, other]

        row_parts[app, r] = acc[...]

        @loop(rows)
        def _(other):
            @pl.when(other != r)
            def _():
                row_copy(app, other).start()

    def row_total(app):
        @loop(rows)
        def _(other):
            @pl.when(other != r)
            def _():
                row_wait(app, other).wait_recv()

        total = row_parts[app, 0]
        for other in range(1, rows):
            total = total + row_parts[app, other]
        return total

    in_second = (lane >= vecs) & (lane < 2 * vecs)

    def first_part(matrix):
        return jnp.where(lane < vecs, matrix, 0.0)

    def second_part(matrix):
        return jnp.where(in_second, matrix, 0.0)

    def apply_first(matrix, block):
        return full_dot(first_part(matrix), placed_rows(block, 0), ((1,), (0,)))

    def apply_second(matrix, block):
        return full_dot(second_part(matrix), placed_rows(block, 1), ((1,), (0,)))

    def gram_pair(left, other):
        zero = jnp.zeros((LANES - 2 * vecs, width), F32)
        right = jnp.concatenate([left, other, zero], axis=0)
        return full_dot(left, right, ((1,), (1,))) / length

    def residual_gram(pair):
        part = second_part(pair)
        return pair - full_dot(part, placed_rows(part, 0), ((1,), (1,)))

    def record(k, pair, work, sigma):
        diagonal = pltpu.roll(pair, LANES - vecs, axis=1) + jnp.where(lane == row, sigma, 0.0)
        rec_ref[k, 0] = diagonal[:, :vecs]
        upper = jnp.where(lane >= row, first_part(work), 0.0)
        rec_ref[k, 1] = placed_rows(upper, 0).T[:vecs, :vecs]

    energy = e_ref[...]
    start = x_ref[...]
    zero_block = jnp.zeros_like(start)
    local = gram_pair(start, zero_block) + jnp.where(lane == 2 * vecs, jnp.sum(energy) / length, 0.0)

    split_blocks()
    pl.semaphore_wait(barrier, cols - 1 + rows - 1)
    send_block(0, x_ref)
    gram_start(0, local)
    send_across(0, x_ref)
    gram_middle(0)
    downward(0)
    collect(0)
    pair = gram_end(0)
    sigma = pair[0:1, 2 * vecs : 2 * vecs + 1]
    work = factor_and_inverse(pair, row, lane, vecs)
    current = apply_second(work, start)
    image = apply_second(work, row_total(0) + energy * start)
    w_buf[...] = image - sigma * current

    send_block(1, w_buf)
    shifted = w_buf[...]
    gram_start(1, gram_pair(shifted, current))
    send_across(1, w_buf)
    gram_middle(1)
    downward(1)
    collect(1)
    pair = gram_end(1)
    work = factor_and_inverse(residual_gram(pair), row, lane, vecs)
    following = apply_second(work, shifted - apply_second(pair, current))
    known_image = energy * shifted - apply_second(pair, image)
    known_last = apply_first(work, current) + sigma * following
    last = apply_second(work, row_total(1) + known_image) - known_last
    gram_start(2, gram_pair(last, following))
    record(0, pair, work, sigma)
    gram_middle(2)
    pair = gram_end(2)
    work = factor_and_inverse(residual_gram(pair), row, lane, vecs)
    record(1, pair, work, sigma)
    next_ref[...] = apply_second(work, last - apply_second(pair, following))

    for app in range(ITERS):
        source = x_ref if app == 0 else w_buf

        targets(lambda other: gather_copy(app, source, other).wait_send())

        @loop(slots)
        def _(i):
            @pl.when(is_relayed(i))
            def _():
                relay_copy(app, i).wait_send()

            @pl.when(goes_to_partner(i))
            def _():
                pair_copy(app, i).wait_send()

            @pl.when(is_finished_here(i) | stays_on_chip(i))
            def _():
                across_copy(app, i).wait_send()

        @loop(rows)
        def _(other):
            @pl.when(other != r)
            def _():
                row_copy(app, other).wait_send()

    for k in range(ITERS + 1):
        @loop(group)
        def _(other):
            @pl.when(other != member)
            def _():
                one_copy(k, other).wait_send()

        @loop(teams)
        def _(other):
            @pl.when(other != team)
            def _():
                two_copy(k, other).wait_send()


def solution(mesh):
    rows, cols = mesh.shape["row"], mesh.shape["col"]
    group = 1
    while group * group * 4 <= cols and cols % (2 * group) == 0:
        group *= 2

    def on_device(start_block, energies, hamiltonian):
        vecs, width = start_block.shape
        slots = hamiltonian.shape[0]
        vmem = pl.BlockSpec(memory_space=pltpu.VMEM)
        dma = pltpu.SemaphoreType.DMA
        teams = cols // group
        block = (vecs, width)
        grams = ITERS + 1
        return pl.pallas_call(
            functools.partial(kernel, rows, cols, group),
            out_shape=(
                jax.ShapeDtypeStruct((ITERS, 2, vecs, vecs), F32),
                jax.ShapeDtypeStruct(block, F32),
            ),
            in_specs=[vmem, vmem, pl.BlockSpec(memory_space=pl.ANY)],
            out_specs=(vmem, vmem),
            scratch_shapes=[
                pltpu.VMEM((slots, width, width), F32),
                pltpu.VMEM((slots, width, width), BF16),
                pltpu.VMEM((slots, width, width), BF16),
                pltpu.VMEM((2 * vecs, width), BF16),
                pltpu.VMEM(block, F32),
                pltpu.VMEM((ITERS, slots) + block, F32),
                pltpu.VMEM((ITERS, slots) + block, F32),
                pltpu.VMEM((ITERS, cols // CORES) + block, F32),
                pltpu.VMEM((ITERS, slots) + block, F32),
                pltpu.VMEM(block, F32),
                pltpu.VMEM(block, F32),
                pltpu.VMEM((ITERS, rows) + block, F32),
                pltpu.VMEM((grams, group, vecs, LANES), F32),
                pltpu.VMEM((grams, teams, vecs, LANES), F32),
                dma((slots,)),
                dma((ITERS, cols)),
                dma((ITERS, slots)),
                dma((ITERS, slots)),
                dma((ITERS, slots)),
                dma((ITERS, slots)),
                dma((ITERS, slots)),
                dma((ITERS, cols // CORES)),
                dma((ITERS, rows)),
                dma((ITERS, rows)),
                dma((grams, group)),
                dma((grams, group)),
                dma((grams, teams)),
                dma((grams, teams)),
            ],
            compiler_params=pltpu.CompilerParams(
                collective_id=0, has_side_effects=True, vmem_limit_bytes=56 << 20
            ),
        )(start_block, energies.reshape(1, width), hamiltonian)

    placed = (P(None, "col"), P("col"), P("row", "col", None, None))
    return jax.shard_map(
        on_device, mesh=mesh, in_specs=placed, out_specs=(P(), P(None, "col")), check_vma=False
    )
```
